128 devices in a mesh: grp: 8 (over y, core), scen: 16 (over z, x).
Axes of the slice: x: 4, y: 4, z: 4, core: 2. Of those that a mesh axis runs over, the one named last changes fastest.
Arguments:
- linv: bfloat16 [256, 2048, 2048], P(('grp', 'scen'))
- link: bfloat16 [256, 2048, 512], P(('grp', 'scen')), may hold values from -0.125 to 0.125
- residual_rows: bfloat16 [256, 2048], P(('grp', 'scen')), may hold values from -24 to 24
- active: int32 [256], P(('grp', 'scen')), may hold values from 512 to 2048
- owner: int32 [256], P(('grp', 'scen')), may hold values from 0 to 255, each once
- weights: float32 [256], replicated, may hold values from 0.01 to 0.1
- first_diag: float32 [512], replicated, may hold values from 1 to 10
- first_rhs: float32 [512], replicated, may hold values from -24 to 24
Outputs:
- step_first: float32 [512], replicated
- scenario_newton_step: float32 [256, 2048], P(('grp', 'scen'))
The draws below stay inside these ranges and needn't reach their ends.
All inputs are finite; a program needn't handle non-finite values.
Results may differ from the reference program's by a relative error of at most 0.0075.
Values sent between devices are 32-bit elements; how exact they have to be, the bound alone decides.
No kernel may reach another device: no remote copies, remote signals or barrier semaphores. Data moves between devices by JAX's collectives and lax.ppermute only.
A program may use at most 128 MiB of HBM per device.

```python
import math
import jax
import jax.numpy as jnp
from jax import lax

P_SIZE = 512
M = 2048
ITERS = 2
SCEN = 256


def draw_linv(key, part):
    keys = jax.random.split(jax.random.fold_in(key, 11), SCEN)

    def single(inner):
        first, second = jax.random.split(inner, 2)
        lower = jnp.tril(jax.random.normal(first, (M, M), jnp.float32) * (0.5 / jnp.sqrt(M * 1.0)), -1)
        diagonal = jnp.exp(jax.random.uniform(second, (M,), jnp.float32, jnp.log(0.5), jnp.log(2.0)))
        matrix = lower + jnp.eye(M, dtype=jnp.float32) * diagonal[None, :]
        return matrix.astype(jnp.bfloat16)
    return lax.map(single, keys)


def touch_ends(entries, key, least, high):
    longest = entries.shape.index(max(entries.shape))
    spots = []
    for shift in (0, 1):
        where = [jax.random.randint(jax.random.fold_in(key, axis), (), 0, length) for axis, length in enumerate(entries.shape)]
        where[longest] = (where[longest] + shift) % entries.shape[longest]
        spots.append(tuple(where))
    return entries.at[spots[0]].set(least).at[spots[1]].set(high)


def levels(own_key, dims, cuts, least, high):
    def one(position, parts):
        steps = jax.random.uniform(jax.random.fold_in(jax.random.fold_in(own_key, 6), position), (parts,), jnp.float32, least / len(cuts), high / len(cuts))
        return jnp.repeat(jnp.exp(steps), dims[position] // parts).reshape((-1,) + (1,) * (len(dims) - position - 1))

    gain = one(*cuts[0])
    for cut in cuts[1:]:
        gain = gain * one(*cut)
    return gain


def normal_values(stream_key, dims, spread, reach, shards=(), kind=jnp.bfloat16):
    level = levels(stream_key, dims, shards, -0.22, 0.18) if shards else 1.0
    array = jax.random.normal(stream_key, dims, jnp.float32) * spread * level
    return jnp.minimum(jnp.maximum(array, -reach), reach).astype(kind)


def setup_inputs(seed: int = 0) -> dict:
    streams_of = jax.random.split(jax.random.key(seed), 9)
    linv = draw_linv(jax.random.fold_in(streams_of[8], 71), 0)
    link = normal_values(streams_of[1], (SCEN, M, P_SIZE), M ** -0.5, 0.125, ((0, 128),))
    residual_rows = normal_values(streams_of[2], (SCEN, M), 4.0, 24.0, ((0, 128),))
    active = touch_ends(jax.random.randint(streams_of[3], (SCEN,), M // 4, M + 1), jax.random.fold_in(streams_of[3], 1), M // 4, M).astype(jnp.int32)
    owner = jax.random.permutation(streams_of[4], SCEN).astype(jnp.int32)
    weights = jnp.clip(jnp.exp(jax.random.uniform(streams_of[5], (SCEN,), jnp.float32, math.log(0.01), math.log(0.1))), 0.01, 0.1)
    first_diag = jnp.clip(jnp.exp(jax.random.uniform(streams_of[6], (P_SIZE,), jnp.float32, math.log(1.0), math.log(10.0))), 1.0, 10.0)
    first_rhs = normal_values(streams_of[7], (P_SIZE,), 4.0, 24.0, (), jnp.float32)
    return {"linv": linv, "link": link, "residual_rows": residual_rows, "active": active, "owner": owner, "weights": weights, "first_diag": first_diag, "first_rhs": first_rhs}


def reference(linv, link, residual_rows, active, owner, weights, first_diag, first_rhs):
    probs = weights[owner]
    rows = jnp.arange(M, dtype=jnp.int32)

    def prepare(matrix, columns, right, count):
        keep = rows < count
        masked = jnp.where(keep[:, None], columns, jnp.zeros_like(columns))
        solved = jnp.dot(matrix, masked, preferred_element_type=jnp.float32).astype(jnp.bfloat16)
        lifted = jnp.dot(matrix, right, preferred_element_type=jnp.float32).astype(jnp.bfloat16)
        return solved, lifted

    def accumulate(carry, entry_element):
        matrix, columns, right, count, weight = entry_element
        solved, lifted = prepare(matrix, columns, right, count)
        gram = jnp.dot(solved.T, solved, preferred_element_type=jnp.float32)
        cross = jnp.dot(lifted, solved, preferred_element_type=jnp.float32)
        return (carry[0] + weight * gram, carry[1] + weight * cross), None

    start = (jnp.zeros((P_SIZE, P_SIZE), jnp.float32), jnp.zeros((P_SIZE,), jnp.float32))
    (schur_sum, cross_sum), unused = lax.scan(accumulate, start, (linv, link, residual_rows, active, probs))
    schur = jnp.diag(first_diag) + schur_sum
    vector = first_rhs - cross_sum
    iterate = jnp.zeros_like(vector)
    remain = vector
    direction = vector
    norm_now = jnp.sum(remain * remain)
    for step in range(ITERS):
        image = jnp.dot(schur, direction, precision=lax.Precision.HIGHEST)
        alpha = norm_now / jnp.sum(direction * image)
        iterate = iterate + alpha * direction
        remain = remain - alpha * image
        norm_next = jnp.sum(remain * remain)
        direction = remain + (norm_next / norm_now) * direction
        norm_now = norm_next
    step_first = iterate
    step_bf = step_first.astype(jnp.bfloat16)

    def back_solve(entry_element):
        matrix, columns, right, count = entry_element
        solved, lifted = prepare(matrix, columns, right, count)
        residue = lifted.astype(jnp.float32) - jnp.dot(solved, step_bf, preferred_element_type=jnp.float32)
        return jnp.dot(residue.astype(jnp.bfloat16), matrix, preferred_element_type=jnp.float32)

    scenario_newton_step = lax.map(back_solve, (linv, link, residual_rows, active))
    return step_first, scenario_newton_step
```

```python
import jax
import jax.numpy as jnp
from jax import lax
from jax.experimental import pallas as pl
from jax.experimental.pallas import tpu as pltpu
from jax.sharding import PartitionSpec as P

BOTH = ("grp", "scen")
BLOCK = 256
NT = (((1,), (1,)), ((), ()))
NN = (((1,), (0,)), ((), ()))
TN = (((0,), (0,)), ((), ()))
VMEM_LIMIT = 56 * 1024 * 1024
SMEM_SPEC = pl.BlockSpec(memory_space=pltpu.SMEM)
VMEM_SPEC = pl.BlockSpec(memory_space=pltpu.VMEM)
ANY_SPEC = pl.BlockSpec(memory_space=pl.ANY)


def mul(a, b, dims):
    return lax.dot_general(a, b, dims, preferred_element_type=jnp.float32)


def pieces(row):
    high = row.astype(jnp.bfloat16).astype(jnp.float32)
    rest = row - high
    middle = rest.astype(jnp.bfloat16).astype(jnp.float32)
    low = rest - middle
    width = row.shape[1]
    ids = lax.broadcasted_iota(jnp.int32, (8, width), 0)
    spread = lambda part: jnp.broadcast_to(part, (8, width))
    out = jnp.where(ids == 0, spread(high), jnp.where(ids == 1, spread(middle), jnp.where(ids == 2, spread(low), 0.0)))
    return out.astype(jnp.bfloat16)


def total(rows):
    return jnp.sum(rows, axis=0, keepdims=True)


def block_copies(linv, buffer, sems, count, blocks):
    copies = []
    for s in range(count):
        for i in range(blocks):
            where = (s, pl.ds(i * BLOCK, BLOCK), pl.ds(0, (i + 1) * BLOCK))
            copies.append(pltpu.make_async_copy(linv.at[where], buffer.at[where], sems.at[s, i]))
    return copies


def first_kernel(owner, weights, active, linv, link, right, lift_out, cross_out, lbuf, kbuf, acc, sems, link_sems):
    count, rows, width = link.shape
    blocks = rows // BLOCK
    copies = block_copies(linv, lbuf, sems, count, blocks)
    for copy in copies:
        copy.start()
    links = [pltpu.make_async_copy(link.at[s], kbuf.at[s], link_sems.at[s]) for s in range(count)]
    for copy in links:
        copy.start()
    cross = jnp.zeros((1, width), jnp.float32)
    products = []
    for s in range(count):
        wide = jnp.broadcast_to(right[s].astype(jnp.float32), (8, rows)).astype(jnp.bfloat16)
        acc[s] = jnp.zeros((8, rows), jnp.float32)
        for i in range(blocks):
            copies[s * blocks + i].wait()
            span = (i + 1) * BLOCK
            tile = lbuf[s, pl.ds(i * BLOCK, BLOCK), pl.ds(0, span)]
            lifted = mul(wide[:, :span], tile, NT).astype(jnp.bfloat16)
            acc[s, :, pl.ds(0, span)] += mul(lifted, tile, NN)
        product = acc[s, pl.ds(0, 1), :]
        lift_out[s] = product
        products.append(product)
    ids = lax.broadcasted_iota(jnp.int32, (1, rows), 1)
    for s in range(count):
        links[s].wait()
        kept = jnp.where(ids < active[s], products[s], 0.0)
        cross = cross + weights[owner[s]] * total(mul(pieces(kept), kbuf[s], NN))
    cross_out[...] = jnp.broadcast_to(cross, cross_out.shape)


def gram_kernel(owner, weights, active, linv, link, solved_out, gram_out, lbuf, kbuf, sems, link_sems):
    count, rows, width = link.shape
    blocks = rows // BLOCK
    copies = block_copies(linv, lbuf, sems, count, blocks)
    links = []
    for s in range(count):
        for i in range(blocks):
            where = (s, pl.ds(i * BLOCK, BLOCK))
            links.append(pltpu.make_async_copy(link.at[where], kbuf.at[where], link_sems.at[s, i]))
    for a, b in zip(links, copies):
        a.start()
        b.start()
    for s in range(count):
        for i in range(blocks):
            links[s * blocks + i].wait()
            ids = i * BLOCK + lax.broadcasted_iota(jnp.int32, (BLOCK, width), 0)
            part = kbuf[s, pl.ds(i * BLOCK, BLOCK)]
            kbuf[s, pl.ds(i * BLOCK, BLOCK)] = jnp.where(ids < active[s], part, jnp.zeros_like(part))
            copies[s * blocks + i].wait()
            span = (i + 1) * BLOCK
            tile = lbuf[s, pl.ds(i * BLOCK, BLOCK), pl.ds(0, span)]
            solved_out[s, pl.ds(i * BLOCK, BLOCK)] = mul(tile, kbuf[s, pl.ds(0, span)], NN).astype(jnp.bfloat16)
        gram = weights[owner[s]] * mul(solved_out[s], solved_out[s], TN)
        if s == 0:
            gram_out[...] = gram
        else:
            gram_out[...] += gram


def exact_mul(row, matrix):
    wide = jnp.broadcast_to(row, (8, row.shape[1]))
    return lax.dot_general(wide, matrix, NN, precision=lax.Precision.HIGHEST, preferred_element_type=jnp.float32)[:1]


def image_kernel(parts, rhs, gram, vector_out, image_out):
    vector = rhs[...] - total(parts[...])
    vector_out[...] = vector
    image_out[...] = jnp.broadcast_to(exact_mul(vector, gram[...]), image_out.shape)


def direction_kernel(parts, diag, vector_in, gram, direction_out, scalars_out, product_out):
    vector = vector_in[...]
    image = diag[...] * vector + total(parts[...])
    dot = lambda a, b: jnp.sum(a * b, axis=1, keepdims=True)
    norm = dot(vector, vector)
    alpha = norm / dot(vector, image)
    remain = vector - alpha * image
    norm_next = dot(remain, remain)
    direction = remain + (norm_next / norm) * vector
    direction_out[...] = direction
    wide = lambda value: jnp.broadcast_to(value, (1, 128))
    scalars_out[pl.ds(0, 1)] = wide(alpha)
    scalars_out[pl.ds(1, 1)] = wide(norm_next)
    scalars_out[pl.ds(2, 1)] = wide(dot(direction * diag[...], direction))
    product_out[...] = jnp.broadcast_to(dot(exact_mul(direction, gram[...]), direction), product_out.shape)


def back_kernel(linv, solved, row, back_out, lbuf, acc, sems):
    count, rows, width = solved.shape
    blocks = rows // BLOCK
    copies = block_copies(linv, lbuf, sems, count, blocks)
    for copy in copies:
        copy.start()
    split = pieces(row[...])
    for s in range(count):
        acc[s] = jnp.zeros((8, rows), jnp.float32)
        for i in range(blocks):
            forward = total(mul(split, solved[s, pl.ds(i * BLOCK, BLOCK)], NT))
            spread = pieces(forward)
            copies[s * blocks + i].wait()
            span = (i + 1) * BLOCK
            tile = lbuf[s, pl.ds(i * BLOCK, BLOCK), pl.ds(0, span)]
            acc[s, :, pl.ds(0, span)] += mul(spread, tile, NN)
        back_out[s] = total(acc[s])


def last_kernel(parts, scalars, vector, direction, lift, first, second, step_out, out):
    alpha = scalars[pl.ds(0, 1), pl.ds(0, 1)]
    norm = scalars[pl.ds(1, 1), pl.ds(0, 1)]
    bend = total(parts[...])[:, :1] + scalars[pl.ds(2, 1), pl.ds(0, 1)]
    beta = norm / bend
    step_out[...] = alpha * vector[...] + beta * direction[...]
    for s in range(out.shape[0]):
        out[pl.ds(s, 1)] = lift[s] - alpha * first[s] - beta * second[s]


def params():
    return pltpu.CompilerParams(vmem_limit_bytes=VMEM_LIMIT)


def body(linv, link, residual_rows, active, owner, weights, first_diag, first_rhs):
    count, rows, width = link.shape
    blocks = rows // BLOCK
    devices = lax.axis_size(BOTH)
    f32 = lambda *dims: jax.ShapeDtypeStruct(dims, jnp.float32)
    l_scratch = pltpu.VMEM((count, rows, rows), jnp.bfloat16)
    k_scratch = pltpu.VMEM((count, rows, width), jnp.bfloat16)
    acc_scratch = pltpu.VMEM((count, 8, rows), jnp.float32)
    block_sems = pltpu.SemaphoreType.DMA((count, blocks))

    def share(rows_of_all):
        return lax.all_to_all(rows_of_all, BOTH, 0, 0, tiled=True)

    right = residual_rows.reshape(count, 1, rows)
    diag = first_diag.reshape(1, width)
    rhs = first_rhs.reshape(1, width)
    lift, cross = pl.pallas_call(
        first_kernel,
        name="first",
        out_shape=(f32(count, 1, rows), f32(devices, width)),
        in_specs=[SMEM_SPEC] * 3 + [ANY_SPEC] * 2 + [VMEM_SPEC],
        out_specs=(VMEM_SPEC, VMEM_SPEC),
        scratch_shapes=[l_scratch, k_scratch, acc_scratch, block_sems, pltpu.SemaphoreType.DMA((count,))],
        compiler_params=params(),
    )(owner, weights, active, linv, link, right)
    cross_parts = share(cross)
    solved, gram = pl.pallas_call(
        gram_kernel,
        name="gram",
        out_shape=(jax.ShapeDtypeStruct((count, rows, width), jnp.bfloat16), f32(width, width)),
        in_specs=[SMEM_SPEC] * 3 + [ANY_SPEC] * 2,
        out_specs=(VMEM_SPEC, VMEM_SPEC),
        scratch_shapes=[l_scratch, k_scratch, block_sems, block_sems],
        compiler_params=params(),
    )(owner, weights, active, linv, link)
    vector, image = pl.pallas_call(
        image_kernel, name="image", out_shape=(f32(1, width), f32(devices, width)), compiler_params=params()
    )(cross_parts, rhs, gram)
    image_parts = share(image)

    def back(row, name):
        return pl.pallas_call(
            back_kernel,
            name=name,
            out_shape=f32(count, 1, rows),
            in_specs=[ANY_SPEC, VMEM_SPEC, VMEM_SPEC],
            out_specs=VMEM_SPEC,
            scratch_shapes=[l_scratch, acc_scratch, block_sems],
            compiler_params=params(),
        )(linv, solved, row)

    first = back(vector, "back_first")
    direction, scalars, product = pl.pallas_call(
        direction_kernel,
        name="direction",
        out_shape=(f32(1, width), f32(3, 128), f32(devices, 128)),
        compiler_params=params(),
    )(image_parts, diag, vector, gram)
    product_parts = share(product)
    second = back(direction, "back_second")
    step, out = pl.pallas_call(
        last_kernel, name="last", out_shape=(f32(1, width), f32(count, rows)), compiler_params=params()
    )(product_parts, scalars, vector, direction, lift, first, second)
    return step.reshape(width), out


def solution(mesh):
    placed = (
        P(BOTH, None, None),
        P(BOTH, None, None),
        P(BOTH, None),
        P(BOTH),
        P(BOTH),
        P(),
        P(),
        P(),
    )
    return jax.shard_map(body, mesh=mesh, in_specs=placed, out_specs=(P(), P(BOTH, None)), check_vma=False)
```

```python
import jax
import jax.numpy as jnp
from jax import lax
from jax.experimental import pallas as pl
from jax.experimental.pallas import tpu as pltpu
from jax.sharding import PartitionSpec as P

BOTH = ("grp", "scen")
BLOCK = 256
LANES = 128
NT = (((1,), (1,)), ((), ()))
NN = (((1,), (0,)), ((), ()))
TN = (((0,), (0,)), ((), ()))
MIB = 1024 * 1024
SMEM_SPEC = pl.BlockSpec(memory_space=pltpu.SMEM)
VMEM_SPEC = pl.BlockSpec(memory_space=pltpu.VMEM)
HBM_SPEC = pl.BlockSpec(memory_space=pltpu.HBM)


def mul(a, b, dims):
    return lax.dot_general(a, b, dims, preferred_element_type=jnp.float32)


def thirds(value):
    high = value.astype(jnp.bfloat16).astype(jnp.float32)
    rest = value - high
    middle = rest.astype(jnp.bfloat16).astype(jnp.float32)
    return high, middle, rest - middle


def pieces(row):
    width = row.shape[1]
    ids = lax.broadcasted_iota(jnp.int32, (8, width), 0)
    high, middle, low = (jnp.broadcast_to(part, (8, width)) for part in thirds(row))
    out = jnp.where(ids == 0, high, jnp.where(ids == 1, middle, jnp.where(ids == 2, low, 0.0)))
    return out.astype(jnp.bfloat16)


def total(rows):
    return jnp.sum(rows, axis=0, keepdims=True)


def folded(row):
    return jnp.concatenate([row[:, i : i + LANES] for i in range(0, row.shape[1], LANES)], axis=0)


def unfolded(tile):
    return jnp.concatenate([tile[i : i + 1] for i in range(tile.shape[0])], axis=1)


def spread(row, out):
    out[...] = jnp.broadcast_to(folded(row)[None], out.shape)


def gathered(parts):
    return unfolded(jnp.sum(parts[...], axis=0))


def block_copy(s, i, linv, factor, sems):
    where = (s, pl.ds(i * BLOCK, BLOCK), pl.ds(0, (i + 1) * BLOCK))
    return pltpu.make_async_copy(linv.at[where], factor.at[where], sems.at[s, i])


def rows_copy(s, i, source, target, sems):
    where = (s, pl.ds(i * BLOCK, BLOCK))
    return pltpu.make_async_copy(source.at[where], target.at[where], sems.at[s, i])


def block_of(factor, s, i):
    return factor[s, pl.ds(i * BLOCK, BLOCK), pl.ds(0, (i + 1) * BLOCK)]


def kept_rows(columns, s, i, limit):
    part = columns[s, pl.ds(i * BLOCK, BLOCK)]
    ids = i * BLOCK + lax.broadcasted_iota(jnp.int32, part.shape, 0)
    return jnp.where(ids < limit, part, jnp.zeros_like(part))


def first_kernel(
    owner_in, weights_in, active_in, right_in, linv, link, lift_out, cross_out, scale_out,
    owner, weights, active, right, acc, factor, columns, small_sems, sems, link_sems,
):
    count, rows, width = columns.shape
    small = [
        pltpu.make_async_copy(a, b, small_sems.at[i])
        for i, (a, b) in enumerate([(right_in, right), (owner_in, owner), (weights_in, weights), (active_in, active)])
    ]
    for copy in small:
        copy.start()
    steps = [(0, (7,)), (0, (6, 5)), (0, (4, 3, 2, 1, 0)), (1, (7,)), (1, (6, 5)), (1, (4, 3)), (1, (2, 1, 0))]
    for s, group in steps:
        for i in group:
            block_copy(s, i, linv, factor, sems).start()
        for i in group:
            rows_copy(s, i, link, columns, link_sems).start()
    for copy in small:
        copy.wait()
    wide_right = right[...].astype(jnp.float32)
    wide = [jnp.broadcast_to(wide_right[s : s + 1], (8, rows)).astype(jnp.bfloat16) for s in range(count)]
    crosses = [jnp.zeros((8, width), jnp.float32) for s in range(count)]
    for s in range(count):
        acc[s] = jnp.zeros((8, rows), jnp.float32)

    def finish(step, lifted):
        s, group = step
        for i, row in zip(group, lifted):
            acc[s, :, pl.ds(0, (i + 1) * BLOCK)] += mul(row, block_of(factor, s, i), NN)
        for i in group:
            product = acc[s, pl.ds(0, 1), pl.ds(i * BLOCK, BLOCK)]
            crosses[s] = crosses[s] + mul(pieces(product), kept_rows(columns, s, i, active[s]), NN)

    before = None
    for step in steps:
        s, group = step
        for i in group:
            block_copy(s, i, linv, factor, sems).wait()
            rows_copy(s, i, link, columns, link_sems).wait()
        lifted = [mul(wide[s][:, : (i + 1) * BLOCK], block_of(factor, s, i), NT).astype(jnp.bfloat16) for i in group]
        if before:
            finish(*before)
        before = step, lifted
    finish(*before)
    cross = jnp.zeros((1, width), jnp.float32)
    for s in range(count):
        lift_out[s] = acc[s, pl.ds(0, 1), :]
        scale = weights[owner[s]]
        scale_out[s] = jnp.full((1, LANES), scale)
        cross = cross + scale * total(crosses[s])
    spread(cross, cross_out)


def gram_kernel(scale, active, linv, link, solved_out, gram_out, factor, columns, solved, sems, link_sems, out_sems):
    count, rows, width = columns.shape
    steps = [(0, (0, 1, 2, 3)), (0, (4, 5, 6, 7)), (1, (0, 1, 2, 3, 4, 5, 6, 7))]
    for s, group in steps:
        for i in group:
            rows_copy(s, i, link, columns, link_sems).start()
            block_copy(s, i, linv, factor, sems).start()
    for s, group in steps:
        for i in group:
            rows_copy(s, i, link, columns, link_sems).wait()
            block_copy(s, i, linv, factor, sems).wait()
        for i in group:
            columns[s, pl.ds(i * BLOCK, BLOCK)] = kept_rows(columns, s, i, active[s])
        for i in group:
            product = mul(block_of(factor, s, i), columns[s, pl.ds(0, (i + 1) * BLOCK)], NN)
            solved[s, pl.ds(i * BLOCK, BLOCK)] = product.astype(jnp.bfloat16)
        for i in group:
            rows_copy(s, i, solved, solved_out, out_sems).start()
    half = width // 2
    quads = []
    for top, left in ((0, 0), (0, half), (half, half)):
        quad = jnp.zeros((half, half), jnp.float32)
        for s in range(count):
            quad = quad + scale[s][:, :1] * mul(solved[s, :, pl.ds(top, half)], solved[s, :, pl.ds(left, half)], TN)
        quads.append(quad)
    gram = jnp.concatenate(
        [jnp.concatenate([quads[0], quads[1]], axis=1), jnp.concatenate([quads[1].T, quads[2]], axis=1)], axis=0
    )
    for i, part in enumerate(thirds(gram)):
        gram_out[i] = part.astype(jnp.bfloat16)
    for s in range(count):
        for i in range(rows // BLOCK):
            rows_copy(s, i, solved, solved_out, out_sems).wait()


def gram_times(row, gram):
    left = pieces(row)
    return total(mul(left, gram[0], NN) + mul(left, gram[1], NN) + mul(left, gram[2], NN))


def image_kernel(parts, rhs, gram, vector_out, image_out):
    vector = rhs[...] - gathered(parts)
    vector_out[...] = vector
    spread(gram_times(vector, gram), image_out)


def direction_kernel(parts, diag, vector_in, gram, after, direction_out, scalars_out, product_out):
    vector = vector_in[...]
    image = diag[...] * vector + gathered(parts)
    dot = lambda a, b: jnp.sum(a * b, axis=1, keepdims=True)
    norm = dot(vector, vector)
    alpha = norm / dot(vector, image)
    remain = vector - alpha * image
    norm_next = dot(remain, remain)
    direction = remain + (norm_next / norm) * vector
    direction_out[...] = direction
    wide = lambda value: jnp.broadcast_to(value, (1, LANES))
    scalars_out[pl.ds(0, 1)] = wide(alpha)
    scalars_out[pl.ds(1, 1)] = wide(norm_next)
    scalars_out[pl.ds(2, 1)] = wide(dot(direction * diag[...], direction))
    product_out[...] = jnp.broadcast_to(wide(dot(gram_times(direction, gram), direction))[None], product_out.shape)


def back_kernel(linv, solved_in, row, back_out, factor, solved, acc, sems, in_sems):
    count, rows, width = solved.shape
    blocks = rows // BLOCK
    groups = [tuple(range(blocks // 2)), tuple(range(blocks // 2, blocks))]
    for s in range(count):
        for group in groups:
            for i in group:
                rows_copy(s, i, solved_in, solved, in_sems).start()
                block_copy(s, i, linv, factor, sems).start()
    split = pieces(row[...])
    for s in range(count):
        acc[...] = jnp.zeros_like(acc)
        for group in groups:
            for i in group:
                rows_copy(s, i, solved_in, solved, in_sems).wait()
                block_copy(s, i, linv, factor, sems).wait()
            forward = [total(mul(split, solved[s, pl.ds(i * BLOCK, BLOCK)], NT)) for i in group]
            for i, part in zip(group, forward):
                acc[:, pl.ds(0, (i + 1) * BLOCK)] += mul(pieces(part), block_of(factor, s, i), NN)
        back_out[s] = total(acc[...])


def last_kernel(parts, scalars, vector, direction, lift, first, second, step_out, out):
    alpha = scalars[pl.ds(0, 1), pl.ds(0, 1)]
    norm = scalars[pl.ds(1, 1), pl.ds(0, 1)]
    bend = jnp.sum(parts[...], axis=0)[:, :1] + scalars[pl.ds(2, 1), pl.ds(0, 1)]
    beta = norm / bend
    step_out[...] = alpha * vector[...] + beta * direction[...]
    for s in range(out.shape[0]):
        out[pl.ds(s, 1)] = lift[s] - alpha * first[s] - beta * second[s]


def placed(array, spec):
    if spec is SMEM_SPEC:
        return array
    return pltpu.with_memory_space_constraint(array, spec.memory_space)


def kernel(fn, name, outs, scratch=(), specs=None, outs_specs=None, mib=8):
    def call(*args):
        return pl.pallas_call(
            fn,
            name=name,
            out_shape=outs,
            in_specs=specs or [VMEM_SPEC] * len(args),
            out_specs=outs_specs or jax.tree.map(lambda _: VMEM_SPEC, outs),
            scratch_shapes=scratch,
            compiler_params=pltpu.CompilerParams(vmem_limit_bytes=mib * MIB),
        )(*[placed(a, specs[i] if specs else VMEM_SPEC) for i, a in enumerate(args)])

    return call


def body(linv, link, residual_rows, active, owner, weights, first_diag, first_rhs):
    count, rows, width = link.shape
    blocks = rows // BLOCK
    devices = lax.axis_size(BOTH)
    f32 = lambda *dims: pltpu.VMEM(dims, jnp.float32)
    bf16 = lambda *dims: pltpu.VMEM(dims, jnp.bfloat16)
    folds = width // LANES

    def share(rows_of_all):
        return lax.all_to_all(rows_of_all, BOTH, 0, 0, tiled=True)

    diag = first_diag.reshape(1, width)
    rhs = first_rhs.reshape(1, width)
    block_sems = pltpu.SemaphoreType.DMA((count, blocks))
    factor = pltpu.VMEM((count, rows, rows), jnp.bfloat16)
    columns = pltpu.VMEM((count, rows, width), jnp.bfloat16)
    lift, cross, scale = kernel(
        first_kernel,
        "first",
        (f32(count, 1, rows), f32(devices, folds, LANES), f32(count, 1, LANES)),
        specs=[HBM_SPEC] * 6,
        scratch=[
            pltpu.SMEM((count,), jnp.int32),
            pltpu.SMEM(weights.shape, jnp.float32),
            pltpu.SMEM((count,), jnp.int32),
            pltpu.VMEM((count, rows), jnp.bfloat16),
            pltpu.VMEM((count, 8, rows), jnp.float32),
            factor,
            columns,
            pltpu.SemaphoreType.DMA((4,)),
            block_sems,
            block_sems,
        ],
        mib=40,
    )(owner, weights, active, residual_rows, linv, link)
    cross_parts = share(cross)
    solved, gram = kernel(
        gram_kernel,
        "gram",
        (pltpu.HBM((count, rows, width), jnp.bfloat16), bf16(3, width, width)),
        specs=[VMEM_SPEC, SMEM_SPEC, HBM_SPEC, HBM_SPEC],
        outs_specs=(HBM_SPEC, VMEM_SPEC),
        scratch=[factor, columns, columns, block_sems, block_sems, block_sems],
        mib=44,
    )(scale, active, linv, link)
    vector, image = kernel(image_kernel, "image", (f32(1, width), f32(devices, folds, LANES)))(cross_parts, rhs, gram)
    image_parts = share(image)

    def back(row, name):
        return kernel(
            back_kernel,
            name,
            f32(count, 1, rows),
            specs=[HBM_SPEC, HBM_SPEC, VMEM_SPEC],
            scratch=[factor, columns, pltpu.VMEM((8, rows), jnp.float32), block_sems, block_sems],
            mib=40,
        )(linv, solved, row)

    first = back(vector, "back_first")
    direction, scalars, product = kernel(direction_kernel, "direction", (f32(1, width), f32(3, LANES), f32(devices, 1, LANES)))(
        image_parts, diag, vector, gram, first
    )
    product_parts = share(product)
    second = back(direction, "back_second")
    step, out = kernel(
        last_kernel, "last", (jax.ShapeDtypeStruct((1, width), jnp.float32), jax.ShapeDtypeStruct((count, rows), jnp.float32))
    )(product_parts, scalars, vector, direction, lift, first, second)
    return step.reshape(width), out


def solution(mesh):
    placed = (
        P(BOTH, None, None),
        P(BOTH, None, None),
        P(BOTH, None),
        P(BOTH),
        P(BOTH),
        P(),
        P(),
        P(),
    )
    return jax.shard_map(body, mesh=mesh, in_specs=placed, out_specs=(P(), P(BOTH, None)), check_vma=False)
```

```python
import jax
import jax.numpy as jnp
from jax import lax
from jax.experimental import pallas as pl
from jax.experimental.pallas import tpu as pltpu
from jax.sharding import PartitionSpec as P

BOTH = ("grp", "scen")
BLOCK = 256
LANES = 128
NT = (((1,), (1,)), ((), ()))
NN = (((1,), (0,)), ((), ()))
TN = (((0,), (0,)), ((), ()))
MIB = 1024 * 1024
STEPS = ((0, (0, 1)), (0, (2, 3)), (0, (4, 5)), (0, (6, 7)), (1, (0, 1, 2, 3)), (1, (4, 5)), (1, (6, 7)))
SMEM_SPEC = pl.BlockSpec(memory_space=pltpu.SMEM)
VMEM_SPEC = pl.BlockSpec(memory_space=pltpu.VMEM)
HBM_SPEC = pl.BlockSpec(memory_space=pltpu.HBM)


def mul(a, b, dims):
    return lax.dot_general(a, b, dims, preferred_element_type=jnp.float32)


def thirds(value):
    high = value.astype(jnp.bfloat16).astype(jnp.float32)
    rest = value - high
    middle = rest.astype(jnp.bfloat16).astype(jnp.float32)
    return high, middle, rest - middle


def pieces(row):
    width = row.shape[1]
    ids = lax.broadcasted_iota(jnp.int32, (8, width), 0)
    high, middle, low = (jnp.broadcast_to(part, (8, width)) for part in thirds(row))
    out = jnp.where(ids == 0, high, jnp.where(ids == 1, middle, jnp.where(ids == 2, low, 0.0)))
    return out.astype(jnp.bfloat16)


def total(rows):
    return jnp.sum(rows, axis=0, keepdims=True)


def folded(row):
    return jnp.concatenate([row[:, i : i + LANES] for i in range(0, row.shape[1], LANES)], axis=0)


def unfolded(tile):
    return jnp.concatenate([tile[i : i + 1] for i in range(tile.shape[0])], axis=1)


def spread(row, out):
    out[...] = jnp.broadcast_to(folded(row)[None], out.shape)


def gathered(parts):
    return unfolded(jnp.sum(parts[...], axis=0))


def block_copy(s, i, linv, factor, sems):
    where = (s, pl.ds(i * BLOCK, BLOCK), pl.ds(0, (i + 1) * BLOCK))
    return pltpu.make_async_copy(linv.at[where], factor.at[where], sems.at[s, i])


def rows_copy(s, i, source, target, sems):
    where = (s, pl.ds(i * BLOCK, BLOCK))
    return pltpu.make_async_copy(source.at[where], target.at[where], sems.at[s, i])


def block_of(factor, s, i):
    return factor[s, pl.ds(i * BLOCK, BLOCK), pl.ds(0, (i + 1) * BLOCK)]


def kept_rows(columns, s, i, limit):
    part = columns[s, pl.ds(i * BLOCK, BLOCK)]
    ids = i * BLOCK + lax.broadcasted_iota(jnp.int32, part.shape, 0)
    return jnp.where(ids < limit, part, jnp.zeros_like(part))


def lift_rows(factor, s, i, wide):
    part = jnp.zeros((BLOCK, LANES), jnp.float32)
    for at in range(0, (i + 1) * BLOCK, LANES):
        tile = factor[s, pl.ds(i * BLOCK, BLOCK), pl.ds(at, LANES)].astype(jnp.float32)
        part = part + tile * wide[:, at : at + LANES]
    return jnp.sum(part, axis=1, keepdims=True)


def first_kernel(
    owner_in, weights_in, active_in, right_in, linv, link, lift_out, cross_out, scale_out, solved_out,
    owner, weights, active, right, factor, columns, solved, small_sems, sems, link_sems, out_sems,
):
    count, rows, width = columns.shape
    small = [
        pltpu.make_async_copy(a, b, small_sems.at[i])
        for i, (a, b) in enumerate([(right_in, right), (owner_in, owner), (weights_in, weights), (active_in, active)])
    ]
    for copy in small:
        copy.start()
    steps = STEPS
    for s, group in steps:
        for i in group:
            rows_copy(s, i, link, columns, link_sems).start()
            block_copy(s, i, linv, factor, sems).start()
    for copy in small:
        copy.wait()
    wide_right = right[...].astype(jnp.float32)
    crosses = [jnp.zeros((8, width), jnp.float32) for s in range(count)]

    def finish(step, lifted):
        s, group = step
        for i, column in zip(group, lifted):
            rounded = solved[s, pl.ds(i * BLOCK, BLOCK)].astype(jnp.float32) * column
            crosses[s] = crosses[s] + jnp.sum(rounded.reshape(BLOCK // 8, 8, width), axis=0)
            rows_copy(s, i, solved, solved_out, out_sems).start()

    before = None
    for step in steps:
        s, group = step
        for i in group:
            rows_copy(s, i, link, columns, link_sems).wait()
            block_copy(s, i, linv, factor, sems).wait()
        for i in group:
            columns[s, pl.ds(i * BLOCK, BLOCK)] = kept_rows(columns, s, i, active[s])
        lifted = []
        for i in group:
            product = mul(block_of(factor, s, i), columns[s, pl.ds(0, (i + 1) * BLOCK)], NN)
            solved[s, pl.ds(i * BLOCK, BLOCK)] = product.astype(jnp.bfloat16)
            column = lift_rows(factor, s, i, wide_right[s : s + 1]).astype(jnp.bfloat16).astype(jnp.float32)
            lifted.append(column)
            lift_out[s, :, pl.ds(i * BLOCK, BLOCK)] = jnp.broadcast_to(column, (BLOCK, LANES)).T[:1]
        if before:
            finish(*before)
        before = step, lifted
    finish(*before)
    cross = jnp.zeros((1, width), jnp.float32)
    for s in range(count):
        scale = weights[owner[s]]
        scale_out[s] = jnp.full((1, LANES), scale)
        cross = cross + scale * total(crosses[s])
    spread(cross, cross_out)
    for s, group in steps:
        for i in group:
            rows_copy(s, i, solved, solved_out, out_sems).wait()


def gram_kernel(scale, solved_in, gram_out, solved, sems):
    count, rows, width = solved.shape
    copies = [pltpu.make_async_copy(solved_in.at[s], solved.at[s], sems.at[s]) for s in range(count)]
    for copy in copies:
        copy.start()
    half = width // 2
    spots = ((0, 0), (0, half), (half, half))
    quads = [jnp.zeros((half, half), jnp.float32) for _ in spots]
    for s in range(count):
        copies[s].wait()
        for k, (top, left) in enumerate(spots):
            quads[k] = quads[k] + scale[s][:, :1] * mul(solved[s, :, pl.ds(top, half)], solved[s, :, pl.ds(left, half)], TN)
    gram = jnp.concatenate(
        [jnp.concatenate([quads[0], quads[1]], axis=1), jnp.concatenate([quads[1].T, quads[2]], axis=1)], axis=0
    )
    for i, part in enumerate(thirds(gram)):
        gram_out[i] = part.astype(jnp.bfloat16)


def gram_times(row, gram):
    left = pieces(row)
    return total(mul(left, gram[0], NN) + mul(left, gram[1], NN) + mul(left, gram[2], NN))


def image_kernel(parts, rhs, gram, vector_out, image_out):
    vector = rhs[...] - gathered(parts)
    vector_out[...] = vector
    spread(gram_times(vector, gram), image_out)


def direction_kernel(parts, diag, vector_in, gram, direction_out, scalars_out, product_out):
    vector = vector_in[...]
    image = diag[...] * vector + gathered(parts)
    dot = lambda a, b: jnp.sum(a * b, axis=1, keepdims=True)
    norm = dot(vector, vector)
    alpha = norm / dot(vector, image)
    remain = vector - alpha * image
    norm_next = dot(remain, remain)
    direction = remain + (norm_next / norm) * vector
    direction_out[...] = direction
    wide = lambda value: jnp.broadcast_to(value, (1, LANES))
    scalars_out[pl.ds(0, 1)] = wide(alpha)
    scalars_out[pl.ds(1, 1)] = wide(norm_next)
    scalars_out[pl.ds(2, 1)] = wide(dot(direction * diag[...], direction))
    product_out[...] = jnp.broadcast_to(wide(dot(gram_times(direction, gram), direction))[None], product_out.shape)


def back_kernel(linv, solved_in, lift, vector, direction, back_out, factor, solved, acc, sems, in_sems):
    count, rows, width = solved.shape
    blocks = rows // BLOCK
    groups = [tuple(range(blocks // 2)), tuple(range(blocks // 2, blocks))]
    for s in range(count):
        for group in groups:
            for i in group:
                rows_copy(s, i, solved_in, solved, in_sems).start()
                block_copy(s, i, linv, factor, sems).start()
    left = jnp.concatenate([pieces(vector[...]), pieces(direction[...])], axis=0)
    ids = lax.broadcasted_iota(jnp.int32, (8, BLOCK), 0)

    def stacked(products, row):
        first = [jnp.broadcast_to(part, (8, BLOCK)) for part in thirds(total(products[:8]))]
        second = [jnp.broadcast_to(part, (8, BLOCK)) for part in thirds(total(products[8:]))]
        out = jnp.broadcast_to(row, (8, BLOCK))
        for k, part in enumerate(first + second):
            out = jnp.where(ids == k + 1, part, out)
        return jnp.where(ids < 7, out, 0.0).astype(jnp.bfloat16)

    for s in range(count):
        acc[...] = jnp.zeros_like(acc)
        for group in groups:
            for i in group:
                rows_copy(s, i, solved_in, solved, in_sems).wait()
                block_copy(s, i, linv, factor, sems).wait()
            products = [mul(left, solved[s, pl.ds(i * BLOCK, BLOCK)], NT) for i in group]
            for i, product in zip(group, products):
                row = lift[s, :, pl.ds(i * BLOCK, BLOCK)]
                acc[:, pl.ds(0, (i + 1) * BLOCK)] += mul(stacked(product, row), block_of(factor, s, i), NN)
        back_out[s] = acc[...]


def last_kernel(parts, scalars, vector, direction, back, step_out, out):
    alpha = scalars[pl.ds(0, 1), pl.ds(0, 1)]
    norm = scalars[pl.ds(1, 1), pl.ds(0, 1)]
    bend = jnp.sum(parts[...], axis=0)[:, :1] + scalars[pl.ds(2, 1), pl.ds(0, 1)]
    beta = norm / bend
    step_out[...] = alpha * vector[...] + beta * direction[...]
    for s in range(out.shape[0]):
        rows = back[s]
        out[pl.ds(s, 1)] = rows[0:1] - alpha * total(rows[1:4]) - beta * total(rows[4:7])


def placed(array, spec):
    if spec is SMEM_SPEC:
        return array
    return pltpu.with_memory_space_constraint(array, spec.memory_space)


def kernel(fn, name, outs, scratch=(), specs=None, outs_specs=None, mib=8):
    def call(*args):
        return pl.pallas_call(
            fn,
            name=name,
            out_shape=outs,
            in_specs=specs or [VMEM_SPEC] * len(args),
            out_specs=outs_specs or jax.tree.map(lambda _: VMEM_SPEC, outs),
            scratch_shapes=scratch,
            compiler_params=pltpu.CompilerParams(vmem_limit_bytes=mib * MIB),
        )(*[placed(a, specs[i] if specs else VMEM_SPEC) for i, a in enumerate(args)])

    return call


def body(linv, link, residual_rows, active, owner, weights, first_diag, first_rhs):
    count, rows, width = link.shape
    blocks = rows // BLOCK
    devices = lax.axis_size(BOTH)
    f32 = lambda *dims: pltpu.VMEM(dims, jnp.float32)
    bf16 = lambda *dims: pltpu.VMEM(dims, jnp.bfloat16)
    folds = width // LANES

    def share(rows_of_all):
        return lax.all_to_all(rows_of_all, BOTH, 0, 0, tiled=True)

    diag = first_diag.reshape(1, width)
    rhs = first_rhs.reshape(1, width)
    block_sems = pltpu.SemaphoreType.DMA((count, blocks))
    factor = pltpu.VMEM((count, rows, rows), jnp.bfloat16)
    columns = pltpu.VMEM((count, rows, width), jnp.bfloat16)
    lift, cross, scale, solved = kernel(
        first_kernel,
        "first",
        (
            f32(count, 1, rows),
            f32(devices, folds, LANES),
            f32(count, 1, LANES),
            pltpu.HBM((count, rows, width), jnp.bfloat16),
        ),
        specs=[HBM_SPEC] * 6,
        outs_specs=(VMEM_SPEC, VMEM_SPEC, VMEM_SPEC, HBM_SPEC),
        scratch=[
            pltpu.SMEM((count,), jnp.int32),
            pltpu.SMEM(weights.shape, jnp.float32),
            pltpu.SMEM((count,), jnp.int32),
            pltpu.VMEM((count, rows), jnp.bfloat16),
            factor,
            columns,
            columns,
            pltpu.SemaphoreType.DMA((4,)),
            block_sems,
            block_sems,
            block_sems,
        ],
        mib=44,
    )(owner, weights, active, residual_rows, linv, link)
    cross_parts = share(cross)
    gram = kernel(
        gram_kernel,
        "gram",
        bf16(3, width, width),
        specs=[VMEM_SPEC, HBM_SPEC],
        scratch=[columns, pltpu.SemaphoreType.DMA((count,))],
        mib=24,
    )(scale, solved)
    vector, image = kernel(image_kernel, "image", (f32(1, width), f32(devices, folds, LANES)))(cross_parts, rhs, gram)
    image_parts = share(image)
    direction, scalars, product = kernel(direction_kernel, "direction", (f32(1, width), f32(3, LANES), f32(devices, 1, LANES)))(
        image_parts, diag, vector, gram
    )
    product_parts = share(product)
    back = kernel(
        back_kernel,
        "back",
        f32(count, 8, rows),
        specs=[HBM_SPEC, HBM_SPEC, VMEM_SPEC, VMEM_SPEC, VMEM_SPEC],
        scratch=[factor, columns, pltpu.VMEM((8, rows), jnp.float32), block_sems, block_sems],
        mib=40,
    )(linv, solved, lift, vector, direction)
    step, out = kernel(
        last_kernel, "last", (jax.ShapeDtypeStruct((1, width), jnp.float32), jax.ShapeDtypeStruct((count, rows), jnp.float32))
    )(product_parts, scalars, vector, direction, back)
    return step.reshape(width), out


def solution(mesh):
    placed = (
        P(BOTH, None, None),
        P(BOTH, None, None),
        P(BOTH, None),
        P(BOTH),
        P(BOTH),
        P(),
        P(),
        P(),
    )
    return jax.shard_map(body, mesh=mesh, in_specs=placed, out_specs=(P(), P(BOTH, None)), check_vma=False)
```

```python
import jax
import jax.numpy as jnp
from jax import lax
from jax.experimental import pallas as pl
from jax.experimental.pallas import tpu as pltpu
from jax.sharding import PartitionSpec as P

BOTH = ("grp", "scen")
BLOCK = 256
LANES = 128
NT = (((1,), (1,)), ((), ()))
NN = (((1,), (0,)), ((), ()))
TN = (((0,), (0,)), ((), ()))
MIB = 1024 * 1024
STEPS = ((0, (0, 1)), (0, (2, 3, 4)), (0, (5, 6, 7)), (1, (0, 1, 2, 3)), (1, (4, 5, 6, 7)))
LAG = 2
SMEM_SPEC = pl.BlockSpec(memory_space=pltpu.SMEM)
VMEM_SPEC = pl.BlockSpec(memory_space=pltpu.VMEM)
HBM_SPEC = pl.BlockSpec(memory_space=pltpu.HBM)


def mul(a, b, dims):
    return lax.dot_general(a, b, dims, preferred_element_type=jnp.float32)


def thirds(value):
    high = value.astype(jnp.bfloat16).astype(jnp.float32)
    rest = value - high
    middle = rest.astype(jnp.bfloat16).astype(jnp.float32)
    return high, middle, rest - middle


def pieces(row):
    width = row.shape[1]
    ids = lax.broadcasted_iota(jnp.int32, (8, width), 0)
    high, middle, low = (jnp.broadcast_to(part, (8, width)) for part in thirds(row))
    out = jnp.where(ids == 0, high, jnp.where(ids == 1, middle, jnp.where(ids == 2, low, 0.0)))
    return out.astype(jnp.bfloat16)


def total(rows):
    return jnp.sum(rows, axis=0, keepdims=True)


def folded(row):
    return jnp.concatenate([row[:, i : i + LANES] for i in range(0, row.shape[1], LANES)], axis=0)


def unfolded(tile):
    return jnp.concatenate([tile[i : i + 1] for i in range(tile.shape[0])], axis=1)


def spread(row, out):
    out[...] = jnp.broadcast_to(folded(row)[None], out.shape)


def gathered(parts):
    return unfolded(jnp.sum(parts[...], axis=0))


def block_copy(s, i, linv, factor, sems):
    where = (s, pl.ds(i * BLOCK, BLOCK), pl.ds(0, (i + 1) * BLOCK))
    return pltpu.make_async_copy(linv.at[where], factor.at[where], sems.at[s, i])


def rows_copy(s, i, source, target, sems):
    where = (s, pl.ds(i * BLOCK, BLOCK))
    return pltpu.make_async_copy(source.at[where], target.at[where], sems.at[s, i])


def block_of(factor, s, i):
    return factor[s, pl.ds(i * BLOCK, BLOCK), pl.ds(0, (i + 1) * BLOCK)]


def kept_rows(columns, s, i, limit):
    part = columns[s, pl.ds(i * BLOCK, BLOCK)]
    ids = i * BLOCK + lax.broadcasted_iota(jnp.int32, part.shape, 0)
    return jnp.where(ids < limit, part, jnp.zeros_like(part))


def lift_rows(factor, s, i, wide):
    part = jnp.zeros((BLOCK, LANES), jnp.float32)
    for at in range(0, (i + 1) * BLOCK, LANES):
        tile = factor[s, pl.ds(i * BLOCK, BLOCK), pl.ds(at, LANES)].astype(jnp.float32)
        part = part + tile * wide[:, at : at + LANES]
    return jnp.sum(part, axis=1, keepdims=True)


def mask_rows(columns, s, i, limit):
    own = pl.ds(i * BLOCK, BLOCK)
    ids = i * BLOCK + lax.broadcasted_iota(jnp.int32, (BLOCK, LANES), 0)
    keep = jnp.where(ids < limit, 1.0, 0.0).astype(jnp.bfloat16)
    for at in range(0, columns.shape[2], LANES):
        columns[s, own, pl.ds(at, LANES)] = columns[s, own, pl.ds(at, LANES)] * keep


def first_kernel(
    owner_in, weights_in, active_in, right_in, linv, link, lift_out, cross_out, scale_out, solved_out,
    owner, weights, active, right, factor, columns, solved, small_sems, sems, link_sems, out_sems,
):
    count, rows, width = columns.shape
    small = [
        pltpu.make_async_copy(a, b, small_sems.at[i])
        for i, (a, b) in enumerate([(active_in, active), (right_in, right), (owner_in, owner), (weights_in, weights)])
    ]
    for copy in small[:2]:
        copy.start()
    for n, (s, group) in enumerate(STEPS):
        for i in group:
            rows_copy(s, i, link, columns, link_sems).start()
            block_copy(s, i, linv, factor, sems).start()
        if n == 0:
            for copy in small[2:]:
                copy.start()
    wide_right = None
    crosses = [jnp.zeros((8, width), jnp.float32) for s in range(count)]

    def lift(s, i, product):
        column = lift_rows(factor, s, i, wide_right[s : s + 1]).astype(jnp.bfloat16).astype(jnp.float32)
        lift_out[s, :, pl.ds(i * BLOCK, BLOCK)] = jnp.broadcast_to(column, (BLOCK, LANES)).T[:1]
        if product is None:
            product = solved[s, pl.ds(i * BLOCK, BLOCK)].astype(jnp.float32)
        crosses[s] = crosses[s] + jnp.sum((product * column).reshape(BLOCK // 8, 8, width), axis=0)

    waiting = []
    for n, (s, group) in enumerate(STEPS):
        for i in group:
            rows_copy(s, i, link, columns, link_sems).wait()
            block_copy(s, i, linv, factor, sems).wait()
        if n == 0:
            small[0].wait()
        if n == LAG:
            small[1].wait()
            wide_right = right[...].astype(jnp.float32)
        for i in group:
            mask_rows(columns, s, i, active[s])
        for i in group:
            product = mul(block_of(factor, s, i), columns[s, pl.ds(0, (i + 1) * BLOCK)], NN)
            solved[s, pl.ds(i * BLOCK, BLOCK)] = product.astype(jnp.bfloat16)
            rows_copy(s, i, solved, solved_out, out_sems).start()
            if n < LAG:
                waiting.append((s, i))
            else:
                lift(s, i, product)
        if n == LAG:
            for late in waiting:
                lift(*late, None)
    for copy in small[2:]:
        copy.wait()
    cross = jnp.zeros((1, width), jnp.float32)
    for s in range(count):
        scale = weights[owner[s]]
        scale_out[s] = jnp.full((1, LANES), scale)
        cross = cross + scale * total(crosses[s])
    spread(cross, cross_out)
    for s, group in STEPS:
        for i in group:
            rows_copy(s, i, solved, solved_out, out_sems).wait()


def gram_kernel(scale, solved_in, gram_out, solved, sems):
    count, rows, width = solved.shape
    copies = [pltpu.make_async_copy(solved_in.at[s], solved.at[s], sems.at[s]) for s in range(count)]
    for copy in copies:
        copy.start()
    half = width // 2
    spots = ((0, 0), (0, half), (half, half))
    quads = [jnp.zeros((half, half), jnp.float32) for _ in spots]
    for s in range(count):
        copies[s].wait()
        for k, (top, left) in enumerate(spots):
            quads[k] = quads[k] + scale[s][:, :1] * mul(solved[s, :, pl.ds(top, half)], solved[s, :, pl.ds(left, half)], TN)
    gram = jnp.concatenate(
        [jnp.concatenate([quads[0], quads[1]], axis=1), jnp.concatenate([quads[1].T, quads[2]], axis=1)], axis=0
    )
    for i, part in enumerate(thirds(gram)):
        gram_out[i] = part.astype(jnp.bfloat16)


def gram_times(row, gram):
    left = pieces(row)
    return total(mul(left, gram[0], NN) + mul(left, gram[1], NN) + mul(left, gram[2], NN))


def image_kernel(parts, rhs, gram, vector_out, image_out):
    vector = rhs[...] - gathered(parts)
    vector_out[...] = vector
    spread(gram_times(vector, gram), image_out)


def direction_kernel(parts, diag, vector_in, gram, direction_out, scalars_out, product_out):
    vector = vector_in[...]
    image = diag[...] * vector + gathered(parts)
    dot = lambda a, b: jnp.sum(a * b, axis=1, keepdims=True)
    norm = dot(vector, vector)
    alpha = norm / dot(vector, image)
    remain = vector - alpha * image
    norm_next = dot(remain, remain)
    direction = remain + (norm_next / norm) * vector
    direction_out[...] = direction
    wide = lambda value: jnp.broadcast_to(value, (1, LANES))
    scalars_out[pl.ds(0, 1)] = wide(alpha)
    scalars_out[pl.ds(1, 1)] = wide(norm_next)
    scalars_out[pl.ds(2, 1)] = wide(dot(direction * diag[...], direction))
    product_out[...] = jnp.broadcast_to(wide(dot(gram_times(direction, gram), direction))[None], product_out.shape)


def back_kernel(linv, solved_in, lift, vector, direction, back_out, factor, solved, acc, sems, in_sems):
    count, rows, width = solved.shape
    blocks = rows // BLOCK
    groups = [tuple(range(blocks // 2)), tuple(range(blocks // 2, blocks))]
    for s in range(count):
        for group in groups:
            for i in group:
                rows_copy(s, i, solved_in, solved, in_sems).start()
                block_copy(s, i, linv, factor, sems).start()
    left = jnp.concatenate([pieces(vector[...]), pieces(direction[...])], axis=0)
    ids = lax.broadcasted_iota(jnp.int32, (8, BLOCK), 0)

    def stacked(products, row):
        first = [jnp.broadcast_to(part, (8, BLOCK)) for part in thirds(total(products[:8]))]
        second = [jnp.broadcast_to(part, (8, BLOCK)) for part in thirds(total(products[8:]))]
        out = jnp.broadcast_to(row, (8, BLOCK))
        for k, part in enumerate(first + second):
            out = jnp.where(ids == k + 1, part, out)
        return jnp.where(ids < 7, out, 0.0).astype(jnp.bfloat16)

    for s in range(count):
        acc[...] = jnp.zeros_like(acc)
        for group in groups:
            for i in group:
                rows_copy(s, i, solved_in, solved, in_sems).wait()
                block_copy(s, i, linv, factor, sems).wait()
            products = [mul(left, solved[s, pl.ds(i * BLOCK, BLOCK)], NT) for i in group]
            for i, product in zip(group, products):
                row = lift[s, :, pl.ds(i * BLOCK, BLOCK)]
                acc[:, pl.ds(0, (i + 1) * BLOCK)] += mul(stacked(product, row), block_of(factor, s, i), NN)
        back_out[s] = acc[...]


def last_kernel(parts, scalars, vector, direction, back, step_out, out):
    alpha = scalars[pl.ds(0, 1), pl.ds(0, 1)]
    norm = scalars[pl.ds(1, 1), pl.ds(0, 1)]
    bend = jnp.sum(parts[...], axis=0)[:, :1] + scalars[pl.ds(2, 1), pl.ds(0, 1)]
    beta = norm / bend
    step_out[...] = alpha * vector[...] + beta * direction[...]
    for s in range(out.shape[0]):
        rows = back[s]
        out[pl.ds(s, 1)] = rows[0:1] - alpha * total(rows[1:4]) - beta * total(rows[4:7])


def placed(array, spec):
    if spec is SMEM_SPEC:
        return array
    return pltpu.with_memory_space_constraint(array, spec.memory_space)


def kernel(fn, name, outs, scratch=(), specs=None, outs_specs=None, mib=8):
    def call(*args):
        return pl.pallas_call(
            fn,
            name=name,
            out_shape=outs,
            in_specs=specs or [VMEM_SPEC] * len(args),
            out_specs=outs_specs or jax.tree.map(lambda _: VMEM_SPEC, outs),
            scratch_shapes=scratch,
            compiler_params=pltpu.CompilerParams(vmem_limit_bytes=mib * MIB),
        )(*[placed(a, specs[i] if specs else VMEM_SPEC) for i, a in enumerate(args)])

    return call


def body(linv, link, residual_rows, active, owner, weights, first_diag, first_rhs):
    count, rows, width = link.shape
    blocks = rows // BLOCK
    devices = lax.axis_size(BOTH)
    f32 = lambda *dims: pltpu.VMEM(dims, jnp.float32)
    bf16 = lambda *dims: pltpu.VMEM(dims, jnp.bfloat16)
    folds = width // LANES

    def share(rows_of_all):
        return lax.all_to_all(rows_of_all, BOTH, 0, 0, tiled=True)

    diag = first_diag.reshape(1, width)
    rhs = first_rhs.reshape(1, width)
    block_sems = pltpu.SemaphoreType.DMA((count, blocks))
    factor = pltpu.VMEM((count, rows, rows), jnp.bfloat16)
    columns = pltpu.VMEM((count, rows, width), jnp.bfloat16)
    lift, cross, scale, solved = kernel(
        first_kernel,
        "first",
        (
            f32(count, 1, rows),
            f32(devices, folds, LANES),
            f32(count, 1, LANES),
            pltpu.HBM((count, rows, width), jnp.bfloat16),
        ),
        specs=[HBM_SPEC] * 6,
        outs_specs=(VMEM_SPEC, VMEM_SPEC, VMEM_SPEC, HBM_SPEC),
        scratch=[
            pltpu.SMEM((count,), jnp.int32),
            pltpu.SMEM(weights.shape, jnp.float32),
            pltpu.SMEM((count,), jnp.int32),
            pltpu.VMEM((count, rows), jnp.bfloat16),
            factor,
            columns,
            columns,
            pltpu.SemaphoreType.DMA((4,)),
            block_sems,
            block_sems,
            block_sems,
        ],
        mib=44,
    )(owner, weights, active, residual_rows, linv, link)
    cross_parts = share(cross)
    gram = kernel(
        gram_kernel,
        "gram",
        bf16(3, width, width),
        specs=[VMEM_SPEC, HBM_SPEC],
        scratch=[columns, pltpu.SemaphoreType.DMA((count,))],
        mib=24,
    )(scale, solved)
    vector, image = kernel(image_kernel, "image", (f32(1, width), f32(devices, folds, LANES)))(cross_parts, rhs, gram)
    image_parts = share(image)
    direction, scalars, product = kernel(direction_kernel, "direction", (f32(1, width), f32(3, LANES), f32(devices, 1, LANES)))(
        image_parts, diag, vector, gram
    )
    product_parts = share(product)
    back = kernel(
        back_kernel,
        "back",
        f32(count, 8, rows),
        specs=[HBM_SPEC, HBM_SPEC, VMEM_SPEC, VMEM_SPEC, VMEM_SPEC],
        scratch=[factor, columns, pltpu.VMEM((8, rows), jnp.float32), block_sems, block_sems],
        mib=40,
    )(linv, solved, lift, vector, direction)
    step, out = kernel(
        last_kernel, "last", (jax.ShapeDtypeStruct((1, width), jnp.float32), jax.ShapeDtypeStruct((count, rows), jnp.float32))
    )(product_parts, scalars, vector, direction, back)
    return step.reshape(width), out


def solution(mesh):
    placed = (
        P(BOTH, None, None),
        P(BOTH, None, None),
        P(BOTH, None),
        P(BOTH),
        P(BOTH),
        P(),
        P(),
        P(),
    )
    return jax.shard_map(body, mesh=mesh, in_specs=placed, out_specs=(P(), P(BOTH, None)), check_vma=False)
```

```python
import jax
import jax.numpy as jnp
from jax import lax
from jax.experimental import pallas as pl
from jax.experimental.pallas import tpu as pltpu
from jax.sharding import PartitionSpec as P

BOTH = ("grp", "scen")
BLOCK = 256
LANES = 128
NT = (((1,), (1,)), ((), ()))
NN = (((1,), (0,)), ((), ()))
TN = (((0,), (0,)), ((), ()))
MIB = 1024 * 1024
STEPS = ((0, (0, 1)), (0, (2, 3, 4)), (0, (5, 6, 7)), (1, (0, 1, 2, 3)), (1, (4, 5, 6, 7)))
BACK_STEPS = ((0, (0, 1, 2, 3)), (0, (4, 5, 6, 7)), (1, (0, 1, 2, 3)), (1, (4, 5)), (1, (6, 7)))
LAG = 2
DEPTH = 3
NEAR = 4
SMEM_SPEC = pl.BlockSpec(memory_space=pltpu.SMEM)
VMEM_SPEC = pl.BlockSpec(memory_space=pltpu.VMEM)
HBM_SPEC = pl.BlockSpec(memory_space=pltpu.HBM)


def mul(a, b, dims):
    return lax.dot_general(a, b, dims, preferred_element_type=jnp.float32)


def thirds(value):
    high = value.astype(jnp.bfloat16).astype(jnp.float32)
    rest = value - high
    middle = rest.astype(jnp.bfloat16).astype(jnp.float32)
    return high, middle, rest - middle


def pieces(row):
    width = row.shape[1]
    ids = lax.broadcasted_iota(jnp.int32, (8, width), 0)
    high, middle, low = (jnp.broadcast_to(part, (8, width)) for part in thirds(row))
    out = jnp.where(ids == 0, high, jnp.where(ids == 1, middle, jnp.where(ids == 2, low, 0.0)))
    return out.astype(jnp.bfloat16)


def total(rows):
    return jnp.sum(rows, axis=0, keepdims=True)


def folded(row):
    return jnp.concatenate([row[:, i : i + LANES] for i in range(0, row.shape[1], LANES)], axis=0)


def unfolded(tile):
    return jnp.concatenate([tile[i : i + 1] for i in range(tile.shape[0])], axis=1)


def spread(row, out):
    out[...] = jnp.broadcast_to(folded(row)[None], out.shape)


def gathered(parts):
    return unfolded(jnp.sum(parts[...], axis=0))


def block_copy(s, i, linv, factor, sems):
    where = (s, pl.ds(i * BLOCK, BLOCK), pl.ds(0, (i + 1) * BLOCK))
    return pltpu.make_async_copy(linv.at[where], factor.at[where], sems.at[s, i])


def rows_copy(s, i, source, target, sems):
    where = (s, pl.ds(i * BLOCK, BLOCK))
    return pltpu.make_async_copy(source.at[where], target.at[where], sems.at[s, i])


def block_of(factor, s, i):
    return factor[s, pl.ds(i * BLOCK, BLOCK), pl.ds(0, (i + 1) * BLOCK)]


def kept_rows(columns, s, i, limit):
    part = columns[s, pl.ds(i * BLOCK, BLOCK)]
    ids = i * BLOCK + lax.broadcasted_iota(jnp.int32, part.shape, 0)
    return jnp.where(ids < limit, part, jnp.zeros_like(part))


def lift_rows(factor, s, i, wide):
    part = jnp.zeros((BLOCK, LANES), jnp.float32)
    for at in range(0, (i + 1) * BLOCK, LANES):
        tile = factor[s, pl.ds(i * BLOCK, BLOCK), pl.ds(at, LANES)].astype(jnp.float32)
        part = part + tile * wide[:, at : at + LANES]
    return jnp.sum(part, axis=1, keepdims=True)


def mask_rows(columns, s, i, limit):
    own = pl.ds(i * BLOCK, BLOCK)
    ids = i * BLOCK + lax.broadcasted_iota(jnp.int32, (BLOCK, LANES), 0)
    keep = jnp.where(ids < limit, 1.0, 0.0).astype(jnp.bfloat16)
    for at in range(0, columns.shape[2], LANES):
        columns[s, own, pl.ds(at, LANES)] = columns[s, own, pl.ds(at, LANES)] * keep


def in_turn(steps, copies_of, depth, ready):
    for n in range(min(depth, len(steps))):
        for copy in copies_of(*steps[n]):
            copy.start()
    for n, step in enumerate(steps):
        for copy in copies_of(*step):
            copy.wait()
        if n + depth < len(steps):
            for copy in copies_of(*steps[n + depth]):
                copy.start()
        ready(n, *step)


def first_kernel(
    owner_in, weights_in, active_in, right_in, linv, link, lift_out, cross_out, scale_out, ahead_out, near_out,
    owner, weights, active, right, factor, columns, ahead, small_sems, sems, link_sems, out_sems,
):
    count, rows, width = columns.shape
    small = [
        pltpu.make_async_copy(a, b, small_sems.at[i])
        for i, (a, b) in enumerate([(active_in, active), (right_in, right), (owner_in, owner), (weights_in, weights)])
    ]
    for copy in small:
        copy.start()
    crosses = [jnp.zeros((8, width), jnp.float32) for s in range(count)]
    waiting, sent, rights = [], [], []

    def place(s, i):
        at = s * rows + i * BLOCK
        far = ahead.shape[0]
        return (ahead, pl.ds(at, BLOCK)) if at < far else (near_out, pl.ds(at - far, BLOCK))

    def copies_of(s, group):
        return [rows_copy(s, i, link, columns, link_sems) for i in group] + [block_copy(s, i, linv, factor, sems) for i in group]

    def lift(s, i, product):
        column = lift_rows(factor, s, i, rights[0][s : s + 1]).astype(jnp.bfloat16).astype(jnp.float32)
        lift_out[s, :, pl.ds(i * BLOCK, BLOCK)] = jnp.broadcast_to(column, (BLOCK, LANES)).T[:1]
        if product is None:
            solved, own = place(s, i)
            product = solved[own].astype(jnp.float32)
        crosses[s] = crosses[s] + jnp.sum((product * column).reshape(BLOCK // 8, 8, width), axis=0)

    def ready(n, s, group):
        if n == 0:
            small[0].wait()
        if n == LAG:
            small[1].wait()
            rights.append(right[...].astype(jnp.float32))
        for i in group:
            mask_rows(columns, s, i, active[s])
        for i in group:
            solved, own = place(s, i)
            product = mul(block_of(factor, s, i), columns[s, pl.ds(0, (i + 1) * BLOCK)], NN)
            solved[own] = product.astype(jnp.bfloat16)
            if solved is ahead:
                sent.append(pltpu.make_async_copy(ahead.at[own], ahead_out.at[own], out_sems.at[s, i]))
                sent[-1].start()
            if n < LAG:
                waiting.append((s, i))
            else:
                lift(s, i, product)
        if n == LAG:
            for late in waiting:
                lift(*late, None)

    in_turn(STEPS, copies_of, DEPTH, ready)
    for copy in small[2:]:
        copy.wait()
    cross = jnp.zeros((1, width), jnp.float32)
    for s in range(count):
        scale = weights[owner[s]]
        scale_out[s] = jnp.full((1, LANES), scale)
        cross = cross + scale * total(crosses[s])
    spread(cross, cross_out)
    for copy in sent:
        copy.wait()


def gram_kernel(scale, near, ahead_in, near_copy, gram_out, ahead, sems, out_sem):
    width = ahead.shape[1]
    rows = ahead.shape[0] - near.shape[0]
    spans = (pl.ds(0, rows), pl.ds(rows, near.shape[0]))
    coming = [pltpu.make_async_copy(ahead_in.at[span], ahead.at[span], sems.at[i]) for i, span in enumerate(spans)]
    going = pltpu.make_async_copy(near, near_copy, out_sem)
    for copy in coming:
        copy.start()
    going.start()
    half = width // 2
    spots = ((0, 0), (0, half), (half, half))

    def products(s, solved, span):
        return [
            scale[s][:, :1] * mul(solved[span, pl.ds(top, half)], solved[span, pl.ds(left, half)], TN) for top, left in spots
        ]

    quads = products(1, near, pl.ds(0, near.shape[0]))
    for s in range(2):
        coming[s].wait()
        quads = [a + b for a, b in zip(quads, products(s, ahead, spans[s]))]
    gram = jnp.concatenate(
        [jnp.concatenate([quads[0], quads[1]], axis=1), jnp.concatenate([quads[1].T, quads[2]], axis=1)], axis=0
    )
    for i, part in enumerate(thirds(gram)):
        gram_out[i] = part.astype(jnp.bfloat16)
    going.wait()


def gram_times(row, gram):
    left = pieces(row)
    return total(mul(left, gram[0], NN) + mul(left, gram[1], NN) + mul(left, gram[2], NN))


def image_kernel(parts, rhs, gram, vector_out, image_out):
    vector = rhs[...] - gathered(parts)
    vector_out[...] = vector
    spread(gram_times(vector, gram), image_out)


def direction_kernel(parts, diag, vector_in, gram, direction_out, scalars_out, product_out):
    vector = vector_in[...]
    image = diag[...] * vector + gathered(parts)
    dot = lambda a, b: jnp.sum(a * b, axis=1, keepdims=True)
    norm = dot(vector, vector)
    alpha = norm / dot(vector, image)
    remain = vector - alpha * image
    norm_next = dot(remain, remain)
    direction = remain + (norm_next / norm) * vector
    direction_out[...] = direction
    wide = lambda value: jnp.broadcast_to(value, (1, LANES))
    scalars_out[pl.ds(0, 1)] = wide(alpha)
    scalars_out[pl.ds(1, 1)] = wide(norm_next)
    scalars_out[pl.ds(2, 1)] = wide(dot(direction * diag[...], direction))
    product_out[...] = jnp.broadcast_to(wide(dot(gram_times(direction, gram), direction))[None], product_out.shape)


def back_kernel(linv, ahead_in, near_in, lift, vector, direction, back_out, factor, solved, sems, in_sems):
    count, rows, width = solved.shape
    left = jnp.concatenate([pieces(vector[...]), pieces(direction[...])], axis=0)
    ids = lax.broadcasted_iota(jnp.int32, (8, BLOCK), 0)

    def copies_of(s, group):
        out = []
        for i in group:
            own = pl.ds(i * BLOCK, BLOCK)
            at, far = s * rows + i * BLOCK, ahead_in.shape[0]
            source = ahead_in.at[pl.ds(at, BLOCK)] if at < far else near_in.at[pl.ds(at - far, BLOCK)]
            out.append(pltpu.make_async_copy(source, solved.at[s, own], in_sems.at[s, i]))
            out.append(block_copy(s, i, linv, factor, sems))
        return out

    def stacked(products, row):
        first = [jnp.broadcast_to(part, (8, BLOCK)) for part in thirds(total(products[:8]))]
        second = [jnp.broadcast_to(part, (8, BLOCK)) for part in thirds(total(products[8:]))]
        out = jnp.broadcast_to(row, (8, BLOCK))
        for k, part in enumerate(first + second):
            out = jnp.where(ids == k + 1, part, out)
        return jnp.where(ids < 7, out, 0.0).astype(jnp.bfloat16)

    def ready(n, s, group):
        products = [mul(left, solved[s, pl.ds(i * BLOCK, BLOCK)], NT) for i in group]
        for i, product in zip(group, products):
            row = lift[s, :, pl.ds(i * BLOCK, BLOCK)]
            back_out[s, :, pl.ds(0, (i + 1) * BLOCK)] += mul(stacked(product, row), block_of(factor, s, i), NN)

    back_out[...] = jnp.zeros_like(back_out)
    in_turn(BACK_STEPS, copies_of, DEPTH, ready)


def last_kernel(parts, scalars, vector, direction, back, step_out, out):
    alpha = scalars[pl.ds(0, 1), pl.ds(0, 1)]
    norm = scalars[pl.ds(1, 1), pl.ds(0, 1)]
    bend = jnp.sum(parts[...], axis=0)[:, :1] + scalars[pl.ds(2, 1), pl.ds(0, 1)]
    beta = norm / bend
    step_out[...] = alpha * vector[...] + beta * direction[...]
    for s in range(out.shape[0]):
        rows = back[s]
        out[pl.ds(s, 1)] = rows[0:1] - alpha * total(rows[1:4]) - beta * total(rows[4:7])


def placed(array, spec):
    if spec is SMEM_SPEC:
        return array
    return pltpu.with_memory_space_constraint(array, spec.memory_space)


def kernel(fn, name, outs, scratch=(), specs=None, outs_specs=None, mib=8):
    def call(*args):
        return pl.pallas_call(
            fn,
            name=name,
            out_shape=outs,
            in_specs=specs or [VMEM_SPEC] * len(args),
            out_specs=outs_specs or jax.tree.map(lambda _: VMEM_SPEC, outs),
            scratch_shapes=scratch,
            compiler_params=pltpu.CompilerParams(vmem_limit_bytes=mib * MIB),
        )(*[placed(a, specs[i] if specs else VMEM_SPEC) for i, a in enumerate(args)])

    return call


def body(linv, link, residual_rows, active, owner, weights, first_diag, first_rhs):
    count, rows, width = link.shape
    blocks = rows // BLOCK
    devices = lax.axis_size(BOTH)
    f32 = lambda *dims: pltpu.VMEM(dims, jnp.float32)
    bf16 = lambda *dims: pltpu.VMEM(dims, jnp.bfloat16)
    folds = width // LANES

    def share(rows_of_all):
        return lax.all_to_all(rows_of_all, BOTH, 0, 0, tiled=True)

    diag = first_diag.reshape(1, width)
    rhs = first_rhs.reshape(1, width)
    block_sems = pltpu.SemaphoreType.DMA((count, blocks))
    factor = pltpu.VMEM((count, rows, rows), jnp.bfloat16)
    columns = pltpu.VMEM((count, rows, width), jnp.bfloat16)
    near_rows = NEAR * BLOCK
    ahead_rows = count * rows - near_rows
    ahead_solved = pltpu.VMEM((ahead_rows, width), jnp.bfloat16)
    lift, cross, scale, ahead, near = kernel(
        first_kernel,
        "first",
        (
            f32(count, 1, rows),
            f32(devices, folds, LANES),
            f32(count, 1, LANES),
            pltpu.HBM((ahead_rows, width), jnp.bfloat16),
            bf16(near_rows, width),
        ),
        specs=[HBM_SPEC] * 6,
        outs_specs=(VMEM_SPEC, VMEM_SPEC, VMEM_SPEC, HBM_SPEC, VMEM_SPEC),
        scratch=[
            pltpu.SMEM((count,), jnp.int32),
            pltpu.SMEM(weights.shape, jnp.float32),
            pltpu.SMEM((count,), jnp.int32),
            pltpu.VMEM((count, rows), jnp.bfloat16),
            factor,
            columns,
            ahead_solved,
            pltpu.SemaphoreType.DMA((4,)),
            block_sems,
            block_sems,
            block_sems,
        ],
        mib=40,
    )(owner, weights, active, residual_rows, linv, link)
    cross_parts = share(cross)
    near_copy, gram = kernel(
        gram_kernel,
        "gram",
        (pltpu.HBM((near_rows, width), jnp.bfloat16), bf16(3, width, width)),
        specs=[VMEM_SPEC, VMEM_SPEC, HBM_SPEC],
        outs_specs=(HBM_SPEC, VMEM_SPEC),
        scratch=[ahead_solved, pltpu.SemaphoreType.DMA((2,)), pltpu.SemaphoreType.DMA],
        mib=24,
    )(scale, near, ahead)
    vector, image = kernel(image_kernel, "image", (f32(1, width), f32(devices, folds, LANES)))(cross_parts, rhs, gram)
    image_parts = share(image)
    direction, scalars, product = kernel(direction_kernel, "direction", (f32(1, width), f32(3, LANES), f32(devices, 1, LANES)))(
        image_parts, diag, vector, gram
    )
    product_parts = share(product)
    back = kernel(
        back_kernel,
        "back",
        f32(count, 8, rows),
        specs=[HBM_SPEC] * 3 + [VMEM_SPEC] * 3,
        scratch=[factor, columns, block_sems, block_sems],
        mib=40,
    )(linv, ahead, near_copy, lift, vector, direction)
    step, out = kernel(
        last_kernel, "last", (jax.ShapeDtypeStruct((1, width), jnp.float32), jax.ShapeDtypeStruct((count, rows), jnp.float32))
    )(product_parts, scalars, vector, direction, back)
    return step.reshape(width), out


def solution(mesh):
    placed = (
        P(BOTH, None, None),
        P(BOTH, None, None),
        P(BOTH, None),
        P(BOTH),
        P(BOTH),
        P(),
        P(),
        P(),
    )
    return jax.shard_map(body, mesh=mesh, in_specs=placed, out_specs=(P(), P(BOTH, None)), check_vma=False)
```

```python
import jax
import jax.numpy as jnp
from jax import lax
from jax.experimental import pallas as pl
from jax.experimental.pallas import tpu as pltpu
from jax.sharding import PartitionSpec as P

BOTH = ("grp", "scen")
BLOCK = 256
LANES = 128
NT = (((1,), (1,)), ((), ()))
NN = (((1,), (0,)), ((), ()))
TN = (((0,), (0,)), ((), ()))
MIB = 1024 * 1024
STEPS = ((0, (0, 1)), (0, (2, 3)), (0, (4, 5)), (0, (6, 7)), (1, (0, 1, 2, 3)), (1, (4, 5)), (1, (6,)), (1, (7,)))
BACK_STEPS = ((0, (0, 1, 2, 3)), (0, (4, 5, 6, 7)), (1, (0, 1, 2, 3)), (1, (4, 5)), (1, (6, 7)))
LAG = 2
DEPTH = 4
NEAR = 4
SMEM_SPEC = pl.BlockSpec(memory_space=pltpu.SMEM)
VMEM_SPEC = pl.BlockSpec(memory_space=pltpu.VMEM)
HBM_SPEC = pl.BlockSpec(memory_space=pltpu.HBM)


def mul(a, b, dims):
    return lax.dot_general(a, b, dims, preferred_element_type=jnp.float32)


def thirds(value):
    high = value.astype(jnp.bfloat16).astype(jnp.float32)
    rest = value - high
    middle = rest.astype(jnp.bfloat16).astype(jnp.float32)
    return high, middle, rest - middle


def pieces(row):
    width = row.shape[1]
    ids = lax.broadcasted_iota(jnp.int32, (8, width), 0)
    high, middle, low = (jnp.broadcast_to(part, (8, width)) for part in thirds(row))
    out = jnp.where(ids == 0, high, jnp.where(ids == 1, middle, jnp.where(ids == 2, low, 0.0)))
    return out.astype(jnp.bfloat16)


def total(rows):
    return jnp.sum(rows, axis=0, keepdims=True)


def folded(row):
    return jnp.concatenate([row[:, i : i + LANES] for i in range(0, row.shape[1], LANES)], axis=0)


def unfolded(tile):
    return jnp.concatenate([tile[i : i + 1] for i in range(tile.shape[0])], axis=1)


def spread(row, out):
    out[...] = jnp.broadcast_to(folded(row)[None], out.shape)


def gathered(parts):
    return unfolded(jnp.sum(parts[...], axis=0))


def block_copy(s, i, linv, factor, sems):
    where = (s, pl.ds(i * BLOCK, BLOCK), pl.ds(0, (i + 1) * BLOCK))
    return pltpu.make_async_copy(linv.at[where], factor.at[where], sems.at[s, i])


def rows_copy(s, i, source, target, sems):
    where = (s, pl.ds(i * BLOCK, BLOCK))
    return pltpu.make_async_copy(source.at[where], target.at[where], sems.at[s, i])


def block_of(factor, s, i):
    return factor[s, pl.ds(i * BLOCK, BLOCK), pl.ds(0, (i + 1) * BLOCK)]


def kept_rows(columns, s, i, limit):
    part = columns[s, pl.ds(i * BLOCK, BLOCK)]
    ids = i * BLOCK + lax.broadcasted_iota(jnp.int32, part.shape, 0)
    return jnp.where(ids < limit, part, jnp.zeros_like(part))


def lift_rows(factor, s, i, wide):
    part = jnp.zeros((BLOCK, LANES), jnp.float32)
    for at in range(0, (i + 1) * BLOCK, LANES):
        tile = factor[s, pl.ds(i * BLOCK, BLOCK), pl.ds(at, LANES)].astype(jnp.float32)
        part = part + tile * wide[:, at : at + LANES]
    return jnp.sum(part, axis=1, keepdims=True)


def mask_rows(columns, s, i, limit):
    own = pl.ds(i * BLOCK, BLOCK)
    ids = i * BLOCK + lax.broadcasted_iota(jnp.int32, (BLOCK, LANES), 0)
    keep = jnp.where(ids < limit, 1.0, 0.0).astype(jnp.bfloat16)
    for at in range(0, columns.shape[2], LANES):
        columns[s, own, pl.ds(at, LANES)] = columns[s, own, pl.ds(at, LANES)] * keep


def in_turn(steps, copies_of, depth, ready):
    for n in range(min(depth, len(steps))):
        for copy in copies_of(*steps[n]):
            copy.start()
    for n, step in enumerate(steps):
        for copy in copies_of(*step):
            copy.wait()
        if n + depth < len(steps):
            for copy in copies_of(*steps[n + depth]):
                copy.start()
        ready(n, *step)


def first_kernel(
    owner_in, weights_in, active_in, right_in, linv, link, lift_out, cross_out, scale_out, ahead_out, near_out,
    owner, weights, active, right, factor, columns, ahead, small_sems, sems, link_sems, out_sems,
):
    count, rows, width = columns.shape
    small = [
        pltpu.make_async_copy(a, b, small_sems.at[i])
        for i, (a, b) in enumerate([(active_in, active), (right_in, right), (owner_in, owner), (weights_in, weights)])
    ]
    for copy in small:
        copy.start()
    crosses = [jnp.zeros((8, width), jnp.float32) for s in range(count)]
    waiting, sent, rights = [], [], []

    def place(s, i):
        at = s * rows + i * BLOCK
        far = ahead.shape[0]
        return (ahead, pl.ds(at, BLOCK)) if at < far else (near_out, pl.ds(at - far, BLOCK))

    def copies_of(s, group):
        return [rows_copy(s, i, link, columns, link_sems) for i in group] + [block_copy(s, i, linv, factor, sems) for i in group]

    def lift(s, i, product):
        column = lift_rows(factor, s, i, rights[0][s : s + 1]).astype(jnp.bfloat16).astype(jnp.float32)
        lift_out[s, :, pl.ds(i * BLOCK, BLOCK)] = jnp.broadcast_to(column, (BLOCK, LANES)).T[:1]
        if product is None:
            solved, own = place(s, i)
            product = solved[own].astype(jnp.float32)
        crosses[s] = crosses[s] + jnp.sum((product * column).reshape(BLOCK // 8, 8, width), axis=0)

    def ready(n, s, group):
        if n == 0:
            small[0].wait()
        if n == LAG:
            small[1].wait()
            rights.append(right[...].astype(jnp.float32))
        for i in group:
            mask_rows(columns, s, i, active[s])
        for i in group:
            solved, own = place(s, i)
            product = mul(block_of(factor, s, i), columns[s, pl.ds(0, (i + 1) * BLOCK)], NN)
            solved[own] = product.astype(jnp.bfloat16)
            if solved is ahead:
                sent.append(pltpu.make_async_copy(ahead.at[own], ahead_out.at[own], out_sems.at[s, i]))
                sent[-1].start()
            if n < LAG:
                waiting.append((s, i))
            else:
                lift(s, i, product)
        if n == LAG:
            for late in waiting:
                lift(*late, None)

    in_turn(STEPS, copies_of, DEPTH, ready)
    for copy in small[2:]:
        copy.wait()
    cross = jnp.zeros((1, width), jnp.float32)
    for s in range(count):
        scale = weights[owner[s]]
        scale_out[s] = jnp.full((1, LANES), scale)
        cross = cross + scale * total(crosses[s])
    spread(cross, cross_out)
    for copy in sent:
        copy.wait()


def gram_kernel(scale, near, ahead_in, near_copy, gram_out, ahead, sems, out_sem):
    width = ahead.shape[1]
    rows = ahead.shape[0] - near.shape[0]
    spans = (pl.ds(0, rows), pl.ds(rows, near.shape[0]))
    coming = [pltpu.make_async_copy(ahead_in.at[span], ahead.at[span], sems.at[i]) for i, span in enumerate(spans)]
    going = pltpu.make_async_copy(near, near_copy, out_sem)
    for copy in coming:
        copy.start()
    going.start()
    half = width // 2
    spots = ((0, 0), (0, half), (half, half))

    def products(s, solved, span):
        return [
            scale[s][:, :1] * mul(solved[span, pl.ds(top, half)], solved[span, pl.ds(left, half)], TN) for top, left in spots
        ]

    quads = products(1, near, pl.ds(0, near.shape[0]))
    for s in range(2):
        coming[s].wait()
        quads = [a + b for a, b in zip(quads, products(s, ahead, spans[s]))]
    gram = jnp.concatenate(
        [jnp.concatenate([quads[0], quads[1]], axis=1), jnp.concatenate([quads[1].T, quads[2]], axis=1)], axis=0
    )
    for i, part in enumerate(thirds(gram)):
        gram_out[i] = part.astype(jnp.bfloat16)
    going.wait()


def gram_times(row, gram):
    left = pieces(row)
    return total(mul(left, gram[0], NN) + mul(left, gram[1], NN) + mul(left, gram[2], NN))


def image_kernel(parts, rhs, gram, vector_out, image_out):
    vector = rhs[...] - gathered(parts)
    vector_out[...] = vector
    spread(gram_times(vector, gram), image_out)


def direction_kernel(parts, diag, vector_in, gram, direction_out, scalars_out, product_out):
    vector = vector_in[...]
    image = diag[...] * vector + gathered(parts)
    dot = lambda a, b: jnp.sum(a * b, axis=1, keepdims=True)
    norm = dot(vector, vector)
    alpha = norm / dot(vector, image)
    remain = vector - alpha * image
    norm_next = dot(remain, remain)
    direction = remain + (norm_next / norm) * vector
    direction_out[...] = direction
    wide = lambda value: jnp.broadcast_to(value, (1, LANES))
    scalars_out[pl.ds(0, 1)] = wide(alpha)
    scalars_out[pl.ds(1, 1)] = wide(norm_next)
    scalars_out[pl.ds(2, 1)] = wide(dot(direction * diag[...], direction))
    product_out[...] = jnp.broadcast_to(wide(dot(gram_times(direction, gram), direction))[None], product_out.shape)


def back_kernel(linv, ahead_in, near_in, lift, vector, direction, back_out, factor, solved, sems, in_sems):
    count, rows, width = solved.shape
    left = jnp.concatenate([pieces(vector[...]), pieces(direction[...])], axis=0)
    ids = lax.broadcasted_iota(jnp.int32, (8, BLOCK), 0)

    def copies_of(s, group):
        out = []
        for i in group:
            own = pl.ds(i * BLOCK, BLOCK)
            at, far = s * rows + i * BLOCK, ahead_in.shape[0]
            source = ahead_in.at[pl.ds(at, BLOCK)] if at < far else near_in.at[pl.ds(at - far, BLOCK)]
            out.append(pltpu.make_async_copy(source, solved.at[s, own], in_sems.at[s, i]))
            out.append(block_copy(s, i, linv, factor, sems))
        return out

    def stacked(products, row):
        first = [jnp.broadcast_to(part, (8, BLOCK)) for part in thirds(total(products[:8]))]
        second = [jnp.broadcast_to(part, (8, BLOCK)) for part in thirds(total(products[8:]))]
        out = jnp.broadcast_to(row, (8, BLOCK))
        for k, part in enumerate(first + second):
            out = jnp.where(ids == k + 1, part, out)
        return jnp.where(ids < 7, out, 0.0).astype(jnp.bfloat16)

    def ready(n, s, group):
        products = [mul(left, solved[s, pl.ds(i * BLOCK, BLOCK)], NT) for i in group]
        for i, product in zip(group, products):
            row = lift[s, :, pl.ds(i * BLOCK, BLOCK)]
            back_out[s, :, pl.ds(0, (i + 1) * BLOCK)] += mul(stacked(product, row), block_of(factor, s, i), NN)

    back_out[...] = jnp.zeros_like(back_out)
    in_turn(BACK_STEPS, copies_of, DEPTH, ready)


def last_kernel(parts, scalars, vector, direction, back, step_out, out):
    alpha = scalars[pl.ds(0, 1), pl.ds(0, 1)]
    norm = scalars[pl.ds(1, 1), pl.ds(0, 1)]
    bend = jnp.sum(parts[...], axis=0)[:, :1] + scalars[pl.ds(2, 1), pl.ds(0, 1)]
    beta = norm / bend
    step_out[...] = alpha * vector[...] + beta * direction[...]
    for s in range(out.shape[0]):
        rows = back[s]
        out[pl.ds(s, 1)] = rows[0:1] - alpha * total(rows[1:4]) - beta * total(rows[4:7])


def placed(array, spec):
    if spec is SMEM_SPEC:
        return array
    return pltpu.with_memory_space_constraint(array, spec.memory_space)


def kernel(fn, name, outs, scratch=(), specs=None, outs_specs=None, mib=8):
    def call(*args):
        return pl.pallas_call(
            fn,
            name=name,
            out_shape=outs,
            in_specs=specs or [VMEM_SPEC] * len(args),
            out_specs=outs_specs or jax.tree.map(lambda _: VMEM_SPEC, outs),
            scratch_shapes=scratch,
            compiler_params=pltpu.CompilerParams(vmem_limit_bytes=mib * MIB),
        )(*[placed(a, specs[i] if specs else VMEM_SPEC) for i, a in enumerate(args)])

    return call


def body(linv, link, residual_rows, active, owner, weights, first_diag, first_rhs):
    count, rows, width = link.shape
    blocks = rows // BLOCK
    devices = lax.axis_size(BOTH)
    f32 = lambda *dims: pltpu.VMEM(dims, jnp.float32)
    bf16 = lambda *dims: pltpu.VMEM(dims, jnp.bfloat16)
    folds = width // LANES

    def share(rows_of_all):
        return lax.all_to_all(rows_of_all, BOTH, 0, 0, tiled=True)

    diag = first_diag.reshape(1, width)
    rhs = first_rhs.reshape(1, width)
    block_sems = pltpu.SemaphoreType.DMA((count, blocks))
    factor = pltpu.VMEM((count, rows, rows), jnp.bfloat16)
    columns = pltpu.VMEM((count, rows, width), jnp.bfloat16)
    near_rows = NEAR * BLOCK
    ahead_rows = count * rows - near_rows
    ahead_solved = pltpu.VMEM((ahead_rows, width), jnp.bfloat16)
    lift, cross, scale, ahead, near = kernel(
        first_kernel,
        "first",
        (
            f32(count, 1, rows),
            f32(devices, folds, LANES),
            f32(count, 1, LANES),
            pltpu.HBM((ahead_rows, width), jnp.bfloat16),
            bf16(near_rows, width),
        ),
        specs=[HBM_SPEC] * 6,
        outs_specs=(VMEM_SPEC, VMEM_SPEC, VMEM_SPEC, HBM_SPEC, VMEM_SPEC),
        scratch=[
            pltpu.SMEM((count,), jnp.int32),
            pltpu.SMEM(weights.shape, jnp.float32),
            pltpu.SMEM((count,), jnp.int32),
            pltpu.VMEM((count, rows), jnp.bfloat16),
            factor,
            columns,
            ahead_solved,
            pltpu.SemaphoreType.DMA((4,)),
            block_sems,
            block_sems,
            block_sems,
        ],
        mib=40,
    )(owner, weights, active, residual_rows, linv, link)
    cross_parts = share(cross)
    near_copy, gram = kernel(
        gram_kernel,
        "gram",
        (pltpu.HBM((near_rows, width), jnp.bfloat16), bf16(3, width, width)),
        specs=[VMEM_SPEC, VMEM_SPEC, HBM_SPEC],
        outs_specs=(HBM_SPEC, VMEM_SPEC),
        scratch=[ahead_solved, pltpu.SemaphoreType.DMA((2,)), pltpu.SemaphoreType.DMA],
        mib=24,
    )(scale, near, ahead)
    vector, image = kernel(image_kernel, "image", (f32(1, width), f32(devices, folds, LANES)))(cross_parts, rhs, gram)
    image_parts = share(image)
    direction, scalars, product = kernel(direction_kernel, "direction", (f32(1, width), f32(3, LANES), f32(devices, 1, LANES)))(
        image_parts, diag, vector, gram
    )
    product_parts = share(product)
    back = kernel(
        back_kernel,
        "back",
        f32(count, 8, rows),
        specs=[HBM_SPEC] * 3 + [VMEM_SPEC] * 3,
        scratch=[factor, columns, block_sems, block_sems],
        mib=40,
    )(linv, ahead, near_copy, lift, vector, direction)
    step, out = kernel(
        last_kernel, "last", (jax.ShapeDtypeStruct((1, width), jnp.float32), jax.ShapeDtypeStruct((count, rows), jnp.float32))
    )(product_parts, scalars, vector, direction, back)
    return step.reshape(width), out


def solution(mesh):
    placed = (
        P(BOTH, None, None),
        P(BOTH, None, None),
        P(BOTH, None),
        P(BOTH),
        P(BOTH),
        P(),
        P(),
        P(),
    )
    return jax.shard_map(body, mesh=mesh, in_specs=placed, out_specs=(P(), P(BOTH, None)), check_vma=False)
```
